256 devices in a mesh: lane: 8 (over y, core), node: 32 (over x, z).
Axes of the slice: x: 4, y: 4, z: 8, core: 2. Of those that a mesh axis runs over, the one named last changes fastest.
Arguments:
- source_row: int32 [32768], P(('lane', 'node')), may hold values from 0 to 63, as said below
- time_bucket: int32 [32768], P(('lane', 'node')), may hold values from 0 to 4095
- neighbour_slot: int32 [32768, 10], P(('lane', 'node')), may hold values from 0 to 511, as said below
- neighbour_age: int32 [32768, 10], P(('lane', 'node')), may hold values from 0 to 4095
- neighbour_count: int32 [32768], P(('lane', 'node')), may hold values from 1 to 10, as said below
- request_rows: int32 [8192, 16], P(('lane', 'node')), may hold values from 0 to 63, as said below
- memory_start: float32 [2048, 512], P('node'), may hold values from -6 to 6
- decay_rate: float32 [512], replicated, may hold values from 0.02 to 1
- time_frequency: float32 [128], replicated, may hold values from 0.0005 to 0.5
- time_phase: float32 [128], replicated, may hold values from -3.140625 to 3.140625
- weight_message: float32 [128, 512], replicated, may hold values from -0.5 to 0.5
- weight_query: bfloat16 [512, 1024], replicated, may hold values from -0.25 to 0.25
- weight_keyval: bfloat16 [512, 2048], replicated, may hold values from -0.25 to 0.25
- weight_time: bfloat16 [128, 1024], replicated, may hold values from -0.5 to 0.5
- weight_output: bfloat16 [1024, 1024], replicated, may hold values from -0.1875 to 0.1875
- weight_skip: bfloat16 [512, 1024], replicated, may hold values from -0.25 to 0.25
Outputs:
- embedding: bfloat16 [32768, 1024], P(('lane', 'node'))
- lane_memory: float32 [8, 2048, 512], P('lane', 'node')
The draws below stay inside these ranges and needn't reach their ends.
Inputs may be any that keep to these rules, and one draw needn't show every extreme that they name: `source_row`: every row of a device's partition is the source of at least one of that device's events. Each list of request_rows holds 16 different rows; for each device the lists of the owners are what its neighbour slots refer to, filled in a prefix, and at least one list of every device is used in full. neighbour_slot % 16 lies inside the used prefix of the owner's list of the same device. `neighbour_count`: every device has an event with all 10 neighbours.
All inputs are finite; a program needn't handle non-finite values.
Results may differ from the reference program's by a relative error of at most 0.024.
Values may be sent and summed in bfloat16 or wider, within the bound.
A program may use at most 64 MiB of HBM per device.

```python
import math
import jax
import jax.numpy as jnp
from jax import lax

M = 512
D = 1024
H = 8
TE = 128
K = 10
EV = 128
NODE_DEV = 64
CAP = 16
NODES = 2048
DEVS = 256
EVENTS = 32768
N_LANE = 8
N_NODE = 32


def fill_levels(key):
    levels = jax.random.randint(jax.random.fold_in(key, 101), (DEVS, N_NODE), CAP // 2, CAP + 1)
    owners = jnp.arange(N_NODE, dtype=jnp.int32)[None, :]
    devices = jnp.arange(DEVS, dtype=jnp.int32)[:, None]
    return jnp.where(owners == devices % N_NODE, CAP, levels)


def source_one(single):
    parts_keys = jax.random.split(single, 6)
    cover = jax.random.permutation(parts_keys[0], NODE_DEV).astype(jnp.int32)
    extra_count = EV - NODE_DEV
    first = jax.random.randint(parts_keys[1], (extra_count,), 0, NODE_DEV)
    second = jax.random.randint(parts_keys[2], (extra_count,), 0, NODE_DEV)
    third = jax.random.randint(parts_keys[3], (extra_count,), 0, NODE_DEV)
    hottest = jnp.minimum(jnp.minimum(first, second), third)
    relabel = jax.random.permutation(parts_keys[4], NODE_DEV).astype(jnp.int32)
    extra = relabel[hottest]
    joined = jnp.concatenate([cover, extra.astype(jnp.int32)])
    order = jax.random.permutation(parts_keys[5], EV)
    return joined[order]


def draw_source_row(key, part):
    keys = jax.random.split(jax.random.fold_in(key, 505), DEVS)
    return jax.vmap(source_one)(keys).reshape(EVENTS).astype(jnp.int32)


def draw_request_rows(key, part):
    keys = jax.random.split(jax.random.fold_in(key, 202), DEVS * N_NODE)
    return jax.vmap(lambda single: jax.random.permutation(single, NODE_DEV)[:CAP])(keys).astype(jnp.int32)


def draw_neighbour_slot(key, part):
    levels = fill_levels(key)
    first = jax.random.randint(jax.random.fold_in(key, 303), (EVENTS, K), 0, N_NODE)
    second = jax.random.randint(jax.random.fold_in(key, 304), (EVENTS, K), 0, N_NODE)
    device = (jnp.arange(EVENTS, dtype=jnp.int32) // EV)[:, None]
    owner = (jnp.minimum(first, second) + device) % N_NODE
    limit = levels[device, owner]
    position = jax.random.randint(jax.random.fold_in(key, 305), (EVENTS, K), 0, limit)
    return (owner * CAP + position).astype(jnp.int32)


def draw_neighbour_count(key, part):
    counts = jax.random.randint(jax.random.fold_in(key, 406), (EVENTS,), 1, K + 1)
    first_event = jnp.arange(EVENTS, dtype=jnp.int32) % EV == 0
    return jnp.where(first_event, K, counts).astype(jnp.int32)


def plant(array, key, smallest, high):
    longest = array.shape.index(max(array.shape))
    spots = []
    for shift in (0, 1):
        where = [jax.random.randint(jax.random.fold_in(key, axis), (), 0, length) for axis, length in enumerate(array.shape)]
        where[longest] = (where[longest] + shift) % array.shape[longest]
        spots.append(tuple(where))
    return array.at[spots[0]].set(smallest).at[spots[1]].set(high)


def block_levels(key, shape, pieces, low, top_value):
    factor_of, own = 1.0, jax.random.fold_in(key, 6)
    for dim, blocks in pieces:
        steps = jnp.exp(jax.random.uniform(jax.random.fold_in(own, dim), (blocks,), jnp.float32, low / len(pieces), top_value / len(pieces)))
        factor_of = factor_of * jnp.repeat(steps, shape[dim] // blocks).reshape([-1 if axis == dim else 1 for axis in range(len(shape))])
    return factor_of


def gaussian(key, dims, deviation, most, cuts=(), held_as=jnp.bfloat16):
    loudness = block_levels(key, dims, cuts, -0.22, 0.18) if cuts else 1.0
    entries = jax.random.normal(key, dims, jnp.float32) * deviation * loudness
    return jnp.minimum(jnp.maximum(entries, -most), most).astype(held_as)


def setup_inputs(seed: int = 0) -> dict:
    arg_keys = jax.random.split(jax.random.key(seed), 17)
    return {
        "source_row": draw_source_row(jax.random.fold_in(arg_keys[16], 71), 0),
        "time_bucket": plant(jax.random.randint(arg_keys[1], (EVENTS,), 0, 4096), jax.random.fold_in(arg_keys[1], 1), 0, 4095).astype(jnp.int32),
        "neighbour_slot": draw_neighbour_slot(jax.random.fold_in(arg_keys[16], 71), 0),
        "neighbour_age": plant(jax.random.randint(arg_keys[3], (EVENTS, K), 0, 4096), jax.random.fold_in(arg_keys[3], 1), 0, 4095).astype(jnp.int32),
        "neighbour_count": draw_neighbour_count(jax.random.fold_in(arg_keys[16], 71), 0),
        "request_rows": draw_request_rows(jax.random.fold_in(arg_keys[16], 71), 0),
        "memory_start": gaussian(arg_keys[6], (NODES, M), 1.0, 6.0, ((0, 32),), jnp.float32),
        "decay_rate": jnp.clip(jnp.exp(jax.random.uniform(arg_keys[7], (M,), jnp.float32, math.log(0.02), math.log(1.0))), 0.02, 1.0),
        "time_frequency": jnp.clip(jnp.exp(jax.random.uniform(arg_keys[8], (TE,), jnp.float32, math.log(0.0005), math.log(0.5))), 0.0005, 0.5),
        "time_phase": jnp.clip(jax.random.uniform(arg_keys[9], (TE,), jnp.float32, -3.140625, 3.140625), -3.140625, 3.140625),
        "weight_message": gaussian(arg_keys[10], (TE, M), TE ** -0.5, 0.5, (), jnp.float32),
        "weight_query": gaussian(arg_keys[11], (M, D), M ** -0.5, 0.25),
        "weight_keyval": gaussian(arg_keys[12], (M, 2 * D), M ** -0.5, 0.25),
        "weight_time": gaussian(arg_keys[13], (TE, D), TE ** -0.5, 0.5),
        "weight_output": gaussian(arg_keys[14], (D, D), D ** -0.5, 0.1875),
        "weight_skip": gaussian(arg_keys[15], (M, D), M ** -0.5, 0.25),
    }


def encode(values, time_frequency, time_phase):
    return jnp.cos(values.astype(jnp.float32)[..., None] * time_frequency + time_phase)

def attend(query, own, far, time_keys, counts, weight_dim):
    width = weight_dim
    events = query.shape[0]
    heads = H
    size = width // heads
    keys = (far[:, :, :width].astype(jnp.float32) + time_keys).astype(jnp.bfloat16)
    values = far[:, :, width:]
    query_heads = query.reshape(events, heads, size).astype(jnp.float32)
    key_heads = keys.reshape(events, K, heads, size).astype(jnp.float32)
    value_heads = values.reshape(events, K, heads, size).astype(jnp.float32)
    own_keys = own[:, :width].reshape(events, heads, size).astype(jnp.float32)
    own_values = own[:, width:].reshape(events, heads, size).astype(jnp.float32)
    scale = 1.0 / jnp.sqrt(jnp.float32(size))
    scores = jnp.einsum('ehd,ekhd->ehk', query_heads, key_heads) * scale
    selfish = jnp.einsum('ehd,ehd->eh', query_heads, own_keys) * scale
    valid = jnp.arange(K, dtype=jnp.int32)[None, None, :] < counts[:, None, None]
    scores = jnp.where(valid, scores, -1e+30)
    largest = jnp.maximum(lax.optimization_barrier(jnp.max(scores, axis=-1)), selfish)
    expo = jnp.where(valid, jnp.exp(scores - largest[..., None]), 0.0)
    expo_self = jnp.exp(selfish - largest)
    total = lax.optimization_barrier(jnp.sum(expo, axis=-1)) + expo_self
    weights = (expo / total[..., None]).astype(jnp.bfloat16).astype(jnp.float32)
    weight_self = (expo_self / total).astype(jnp.bfloat16).astype(jnp.float32)
    mixed = jnp.einsum('ehk,ekhd->ehd', weights, value_heads) + weight_self[..., None] * own_values
    return mixed.reshape(events, width).astype(jnp.bfloat16)

def reference(source_row, time_bucket, neighbour_slot, neighbour_age, neighbour_count, request_rows, memory_start, decay_rate, time_frequency, time_phase, weight_message, weight_query, weight_keyval, weight_time, weight_output, weight_skip):
    messages = jnp.dot(encode(time_bucket, time_frequency, time_phase), weight_message, precision=lax.Precision.HIGHEST)
    device = jnp.arange(EVENTS, dtype=jnp.int32) // EV
    lanes = device // N_NODE
    target = lanes * NODES + device % N_NODE * NODE_DEV + source_row
    touches = jax.ops.segment_sum(jnp.ones((EVENTS,), jnp.float32), target, N_LANE * NODES).reshape(N_LANE, NODES)
    summed = jax.ops.segment_sum(messages, target, N_LANE * NODES).reshape(N_LANE, NODES, M)
    state = memory_start
    before_list = []
    after_list = []
    for block in range(N_LANE):
        before_list.append(state)
        state = jnp.exp(-decay_rate[None, :] * touches[block][:, None]) * state + summed[block]
        after_list.append(state)
    lane_memory = jnp.stack(after_list)
    rows_all = jnp.stack(before_list).astype(jnp.bfloat16)
    keyval_table = lax.map(lambda rows: jnp.dot(rows, weight_keyval, preferred_element_type=jnp.float32).astype(jnp.bfloat16), rows_all)
    requests = request_rows.reshape(DEVS, N_NODE, CAP)

    def one_device(inputs):
        index, sources, slots, ages, counts = inputs
        lane_index = index // N_NODE
        rows_lane = lax.dynamic_index_in_dim(rows_all, lane_index, 0, keepdims=False)
        table_lane = lax.dynamic_index_in_dim(keyval_table, lane_index, 0, keepdims=False)
        asked = lax.dynamic_index_in_dim(requests, index, 0, keepdims=False)
        query_in = rows_lane[index % N_NODE * NODE_DEV + sources]
        query = jnp.dot(query_in, weight_query, preferred_element_type=jnp.float32).astype(jnp.bfloat16)
        own = jnp.dot(query_in, weight_keyval, preferred_element_type=jnp.float32).astype(jnp.bfloat16)
        owner = slots // CAP
        chosen = owner * NODE_DEV + asked[owner, slots % CAP]
        far = table_lane[chosen]
        enc_ages = encode(ages, time_frequency, time_phase).astype(jnp.bfloat16).reshape(EV * K, TE)
        time_keys = jnp.dot(enc_ages, weight_time, preferred_element_type=jnp.float32).reshape(EV, K, D)
        attended = attend(query, own, far, time_keys, counts, D)
        result = jnp.dot(attended, weight_output, preferred_element_type=jnp.float32) + jnp.dot(query_in, weight_skip, preferred_element_type=jnp.float32)
        return result.astype(jnp.bfloat16)
    embedding = lax.map(one_device, (jnp.arange(DEVS, dtype=jnp.int32), source_row.reshape(DEVS, EV), neighbour_slot.reshape(DEVS, EV, K), neighbour_age.reshape(DEVS, EV, K), neighbour_count.reshape(DEVS, EV)))
    return (embedding.reshape(EVENTS, D), lane_memory)
```

```python
import functools
import math

import jax
import jax.numpy as jnp
from jax import lax
from jax.experimental import pallas as pl
from jax.experimental.pallas import tpu as pltpu
from jax.sharding import PartitionSpec as P

MESH = pl.DeviceIdType.MESH
HEADS = 8
F32, BF16 = jnp.float32, jnp.bfloat16
EXACT = lax.Precision.HIGHEST
SINE = (0.5, -0.020833322778344154, 0.0002604078035801649, -1.5475785630769678e-06, 5.088033105948853e-09)
TURN_HIGH = 6.28125
TURN_LOW = 2.0 * math.pi - TURN_HIGH
ROUNDER = 12582912.0


def cosine(angle):
    turns = (angle * (0.5 / math.pi) + ROUNDER) - ROUNDER
    rest = (angle - turns * TURN_HIGH) - turns * TURN_LOW
    square = rest * rest
    poly = SINE[4]
    for term in SINE[3::-1]:
        poly = poly * square + term
    half = rest * poly
    return 1.0 - 2.0 * (half * half)


def nn(a, b, precision=None):
    return lax.dot_general(a, b, (((1,), (0,)), ((), ())), precision=precision, preferred_element_type=F32)


def nt(a, b, precision=None):
    return lax.dot_general(a, b, (((1,), (1,)), ((), ())), precision=precision, preferred_element_type=F32)


def tn(a, b):
    return lax.dot_general(a, b, (((0,), (0,)), ((), ())), preferred_element_type=F32)


def kernel(
    lanes, nodes,
    source_ref, bucket_ref, slot_ref, age_ref, count_ref, request_ref, start_ref,
    decay_ref, frequency_ref, phase_ref, message_hbm, query_hbm, keyval_hbm, time_hbm, output_hbm, skip_hbm,
    embedding_ref, memory_ref,
    wm, wq, wkv, wt, wo, ws, weight_sem,
    lane_source, lane_bucket, asked_out, asked_in, send_buf, far,
    summed, touched, enc, slots, timed, acc, scores, table_own, value, score, mix, qk,
    lane_send, lane_recv, ask_send, ask_recv, row_send, row_recv,
):
    lane, node = lax.axis_index("lane"), lax.axis_index("node")
    owned, channels = start_ref.shape
    events, neighbours = slot_ref.shape
    cap = request_ref.shape[1]
    width = wq.shape[1]
    size = width // HEADS
    total = nodes * cap

    loads = [
        pltpu.make_async_copy(source, target, weight_sem.at[i])
        for i, (source, target) in enumerate(
            ((message_hbm, wm), (query_hbm, wq), (keyval_hbm, wkv), (time_hbm, wt), (skip_hbm, ws), (output_hbm, wo))
        )
    ]
    for load in loads:
        load.start()

    barrier = pltpu.get_barrier_semaphore()

    def greet_lane(k, _):
        pl.semaphore_signal(barrier, inc=1, device_id=(lax.rem(lane + k, lanes), node), device_id_type=MESH)
        return 0

    def greet_node(k, _):
        pl.semaphore_signal(barrier, inc=1, device_id=(lane, lax.rem(node + k, nodes)), device_id_type=MESH)
        return 0

    lax.fori_loop(1, lanes, greet_lane, 0)
    lax.fori_loop(1, nodes, greet_node, 0)

    for o in range(nodes):
        asked_out[o, :, 0:cap] = request_ref[o : o + 1, :]
    asked_in[pl.ds(node, 1), :, 0:cap] = asked_out[pl.ds(node, 1), :, 0:cap]
    lane_source[pl.ds(lane, 1)] = source_ref[...][None]
    lane_bucket[pl.ds(lane, 1)] = bucket_ref[...][None]
    te = frequency_ref.shape[1]
    frequency = jnp.broadcast_to(frequency_ref[...], (te, te)).T
    phase = jnp.broadcast_to(phase_ref[...], (te, te)).T
    slots[0:neighbours, :] = slot_ref[...].T
    ages = age_ref[...].T.astype(F32)
    for j in range(neighbours):
        enc[j] = cosine(frequency * ages[j : j + 1, :] + phase)
    node_row = lax.broadcasted_iota(jnp.int32, (owned, events), 0)
    own_member = (node_row == source_ref[...]).astype(F32)
    picker = own_member.T.astype(BF16)

    pl.semaphore_wait(barrier, lanes - 1 + nodes - 1)

    def lane_copies(k):
        to = lax.rem(lane + k, lanes)
        return [
            pltpu.make_async_remote_copy(
                src_ref=ref, dst_ref=held.at[lane], send_sem=lane_send.at[i, k], recv_sem=lane_recv.at[i, k],
                device_id=(to, node), device_id_type=MESH,
            )
            for i, (ref, held) in enumerate(((source_ref, lane_source), (bucket_ref, lane_bucket)))
        ]

    def ask_copy(k):
        to = lax.rem(node + k, nodes)
        return pltpu.make_async_remote_copy(
            src_ref=asked_out.at[to], dst_ref=asked_in.at[node], send_sem=ask_send.at[k], recv_sem=ask_recv.at[k],
            device_id=(lane, to), device_id_type=MESH,
        )

    def row_copy(k):
        to = lax.rem(node + k, nodes)
        return pltpu.make_async_remote_copy(
            src_ref=send_buf.at[to], dst_ref=far.at[node], send_sem=row_send.at[k], recv_sem=row_recv.at[k],
            device_id=(lane, to), device_id_type=MESH,
        )

    def loop(count, body):
        def step(k, _):
            body(k)
            return 0

        lax.fori_loop(1, count, step, 0)

    loop(lanes, lambda k: [copy.start() for copy in lane_copies(k)])
    loop(nodes, lambda k: ask_copy(k).start())
    loop(lanes, lambda k: [copy.wait() for copy in lane_copies(k)])

    loads[0].wait()
    ones = jnp.ones((te, events), BF16)
    sums = []
    for l in range(lanes):
        member = (node_row == lane_source[l]).astype(F32)
        encoded = cosine(frequency * lane_bucket[l].astype(F32) + phase)
        sums.append(nt(member, encoded, EXACT))
        touched[l] = nt(member.astype(BF16), ones)
    summed[...] = nn(jnp.concatenate(sums, axis=0), wm[...], EXACT).reshape(lanes, owned, channels)
    decay = -decay_ref[...]
    state = start_ref[...]

    def after(state, count, added):
        return jnp.exp(decay * jnp.concatenate([count] * (channels // te), axis=1)) * state + added

    for l in range(lanes - 1):
        state = jnp.where(l < lane, after(state, touched[l], summed[l]), state)
    memory_ref[...] = after(state, touched[pl.ds(lane, 1)][0], summed[pl.ds(lane, 1)][0])
    rows = state.astype(BF16)
    table_own[...] = rows

    loop(nodes, lambda k: ask_copy(k).wait())
    asked = jnp.concatenate([asked_in[o, :, :] for o in range(nodes)], axis=0).T
    node_lane = lax.broadcasted_iota(jnp.int32, (cap, owned), 1)
    picks = jnp.concatenate([(asked[0:cap, o : o + 1] == node_lane).astype(F32) for o in range(nodes)], axis=0)
    send_buf[...] = nn(picks.astype(BF16), rows).astype(BF16).reshape(nodes, cap, channels)
    loop(nodes, lambda k: row_copy(k).start())
    far[pl.ds(node, 1)] = send_buf[pl.ds(node, 1)]

    for load in loads[1:]:
        load.wait()
    query = nn(picker, nn(rows, wq[...]).astype(BF16)).astype(BF16)
    query_in = nn(picker, rows).astype(BF16)
    timed[...] = jnp.zeros_like(timed)
    for h in range(HEADS):
        head = query[:, h * size : (h + 1) * size]
        qk[h * events : (h + 1) * events, :] = nt(head, wkv[:, h * size : (h + 1) * size]).astype(BF16)
        spread = nt(wt[:, h * size : (h + 1) * size], head)
        for j in range(neighbours):
            timed[h, j : j + 1, :] = jnp.sum(spread * enc[j], axis=0, keepdims=True)
    value[total : total + owned, :] = nn(rows, wkv[:, width:]).astype(BF16)
    own_score = nt(rows, qk[...])
    scores[...] = jnp.zeros_like(scores)
    for h in range(HEADS):
        scores[h, neighbours : neighbours + 1, :] = jnp.sum(
            own_member * own_score[:, h * events : (h + 1) * events], axis=0, keepdims=True
        )
    acc[...] = jnp.zeros_like(acc)

    loop(nodes, lambda k: row_copy(k).wait())
    table = far[...].reshape(total, channels)
    value[0:total, :] = nn(table, wkv[:, width:]).astype(BF16)
    score[...] = nt(table, qk[...])

    piece = 32
    piece_row = lax.broadcasted_iota(jnp.int32, (piece, events), 0)

    def gather(c, _):
        base = pl.multiple_of(c * piece, piece)
        for j in range(neighbours):
            hit = (piece_row + base) == slots[j : j + 1, :]
            for h in range(HEADS):
                found = jnp.where(hit, score[pl.ds(base, piece), h * events : (h + 1) * events], 0.0)
                acc[h, j] += jnp.sum(found.reshape(piece // 8, 8, events), axis=0)
        return 0

    lax.fori_loop(0, total // piece, gather, 0)
    for h in range(HEADS):
        for j in range(neighbours):
            scores[h, j : j + 1, :] = jnp.sum(acc[h, j], axis=0, keepdims=True)
    logits = (scores[...] + timed[...]) * (1.0 / math.sqrt(size))
    place = lax.broadcasted_iota(jnp.int32, logits.shape, 1)
    valid = (place < count_ref[...][None]) | (place == neighbours)
    logits = jnp.where(valid, logits, -1e30)
    expo = jnp.where(valid, jnp.exp(logits - jnp.max(logits, axis=1, keepdims=True)), 0.0)
    scores[...] = (expo / jnp.sum(expo, axis=1, keepdims=True)).astype(BF16).astype(F32)

    def scatter(c, _):
        base = pl.multiple_of(c * piece, piece)
        hits = [(piece_row + base) == slots[j : j + 1, :] for j in range(neighbours)]
        for h in range(HEADS):
            put = jnp.zeros((piece, events), F32)
            for j in range(neighbours):
                put += jnp.where(hits[j], scores[h, j : j + 1, :], 0.0)
            mix[pl.ds(base, piece), h * events : (h + 1) * events] = put.astype(BF16)
        return 0

    lax.fori_loop(0, total // piece, scatter, 0)
    attended = []
    for h in range(HEADS):
        mix[total : total + owned, h * events : (h + 1) * events] = (
            own_member * scores[h, neighbours : neighbours + 1, :]
        ).astype(BF16)
        attended.append(tn(mix[:, h * events : (h + 1) * events], value[:, h * size : (h + 1) * size]).astype(BF16))
    embedding_ref[...] = (nn(jnp.concatenate(attended, axis=1), wo[...]) + nn(query_in, ws[...])).astype(BF16)


def local(
    source_row, time_bucket, neighbour_slot, neighbour_age, neighbour_count, request_rows, memory_start, decay_rate,
    time_frequency, time_phase, weight_message, weight_query, weight_keyval, weight_time, weight_output, weight_skip,
):
    lanes, nodes = lax.axis_size("lane"), lax.axis_size("node")
    owned, channels = memory_start.shape
    events, neighbours = neighbour_slot.shape
    cap = request_rows.shape[1]
    te, width = weight_time.shape
    total = nodes * cap
    row = lambda x: x.reshape(1, -1)
    vmem = pl.BlockSpec(memory_space=pltpu.VMEM)
    hbm = pl.BlockSpec(memory_space=pl.ANY)
    dma = pltpu.SemaphoreType.DMA
    embedding, memory = pl.pallas_call(
        functools.partial(kernel, lanes, nodes),
        out_shape=(
            jax.ShapeDtypeStruct((events, width), BF16),
            jax.ShapeDtypeStruct((owned, channels), F32),
        ),
        in_specs=[vmem] * 10 + [hbm] * 6,
        out_specs=(vmem, vmem),
        scratch_shapes=[
            pltpu.VMEM(weight_message.shape, F32),
            pltpu.VMEM(weight_query.shape, BF16),
            pltpu.VMEM(weight_keyval.shape, BF16),
            pltpu.VMEM(weight_time.shape, BF16),
            pltpu.VMEM(weight_output.shape, BF16),
            pltpu.VMEM(weight_skip.shape, BF16),
            dma((6,)),
            pltpu.VMEM((lanes, 1, events), jnp.int32),
            pltpu.VMEM((lanes, 1, events), jnp.int32),
            pltpu.VMEM((nodes, 1, 128), jnp.int32),
            pltpu.VMEM((nodes, 1, 128), jnp.int32),
            pltpu.VMEM((nodes, cap, channels), BF16),
            pltpu.VMEM((nodes, cap, channels), BF16),
            pltpu.VMEM((lanes, owned, channels), F32),
            pltpu.VMEM((lanes, owned, te), F32),
            pltpu.VMEM((neighbours, te, events), F32),
            pltpu.VMEM((16, events), jnp.int32),
            pltpu.VMEM((HEADS, 16, events), F32),
            pltpu.VMEM((HEADS, neighbours, 8, events), F32),
            pltpu.VMEM((HEADS, 16, events), F32),
            pltpu.VMEM((owned, channels), BF16),
            pltpu.VMEM((total + owned, width), BF16),
            pltpu.VMEM((total, HEADS * events), F32),
            pltpu.VMEM((total + owned, HEADS * events), BF16),
            pltpu.VMEM((HEADS * events, channels), BF16),
            dma((2, lanes)),
            dma((2, lanes)),
            dma((nodes,)),
            dma((nodes,)),
            dma((nodes,)),
            dma((nodes,)),
        ],
        compiler_params=pltpu.CompilerParams(collective_id=0, has_side_effects=True),
    )(
        row(source_row), row(time_bucket), neighbour_slot, neighbour_age, row(neighbour_count), request_rows,
        memory_start, row(decay_rate), row(time_frequency), row(time_phase), weight_message, weight_query,
        weight_keyval, weight_time, weight_output, weight_skip,
    )
    return embedding, memory[None]


def solution(mesh):
    both, rows = P(("lane", "node")), P(("lane", "node"), None)
    return jax.shard_map(
        local,
        mesh=mesh,
        in_specs=(both, both, rows, rows, both, rows, P("node", None)) + (P(),) * 9,
        out_specs=(rows, P("lane", "node", None)),
        check_vma=False,
    )
```

```python
import functools
import math

import jax
import jax.numpy as jnp
from jax import lax
from jax.experimental import pallas as pl
from jax.experimental.pallas import tpu as pltpu
from jax.sharding import PartitionSpec as P

MESH = pl.DeviceIdType.MESH
HEADS = 8
F32, BF16 = jnp.float32, jnp.bfloat16
EXACT = lax.Precision.HIGHEST
SINE = (0.5, -0.020833322778344154, 0.0002604078035801649, -1.5475785630769678e-06, 5.088033105948853e-09)
TURN_HIGH = 6.28125
TURN_LOW = 2.0 * math.pi - TURN_HIGH
ROUNDER = 12582912.0


def cosine(angle):
    turns = (angle * (0.5 / math.pi) + ROUNDER) - ROUNDER
    rest = (angle - turns * TURN_HIGH) - turns * TURN_LOW
    square = rest * rest
    poly = SINE[4]
    for term in SINE[3::-1]:
        poly = poly * square + term
    half = rest * poly
    return 1.0 - 2.0 * (half * half)


def nn(a, b, precision=None):
    return lax.dot_general(a, b, (((1,), (0,)), ((), ())), precision=precision, preferred_element_type=F32)


def nt(a, b, precision=None):
    return lax.dot_general(a, b, (((1,), (1,)), ((), ())), precision=precision, preferred_element_type=F32)


def tn(a, b):
    return lax.dot_general(a, b, (((0,), (0,)), ((), ())), preferred_element_type=F32)


def kernel(
    lanes, nodes,
    source_hbm, bucket_hbm, request_hbm, frequency_hbm, phase_hbm, age_hbm, slot_hbm, count_hbm, decay_hbm, start_hbm,
    message_hbm, query_hbm, keyval_hbm, time_hbm, skip_hbm,
    attended_ref, base_ref, memory_ref,
    source_ref, bucket_ref, request_ref, frequency_ref, phase_ref, age_ref, slot_ref, count_ref, decay_ref, start_ref,
    wm, wq, wkv, wt, ws, load_sem,
    lane_source, lane_bucket, asked_out, asked_in, send_buf, far,
    summed, touched, enc, timed, acc, scores, table_own, value, score, mix, qk,
    lane_send, lane_recv, ask_send, ask_recv, row_send, row_recv,
):
    lane, node = lax.axis_index("lane"), lax.axis_index("node")
    owned, channels = start_ref.shape
    neighbours, events = slot_ref.shape
    cap = request_ref.shape[0]
    width = wq.shape[1]
    size = width // HEADS
    total = nodes * cap

    sources = (
        source_hbm, bucket_hbm, request_hbm, frequency_hbm, phase_hbm, age_hbm, slot_hbm, count_hbm, decay_hbm,
        start_hbm, message_hbm, query_hbm, keyval_hbm, time_hbm, skip_hbm,
    )
    held = (
        source_ref, bucket_ref, request_ref, frequency_ref, phase_ref, age_ref, slot_ref, count_ref, decay_ref,
        start_ref, wm, wq, wkv, wt, ws,
    )
    loads = [pltpu.make_async_copy(a, b, load_sem.at[i]) for i, (a, b) in enumerate(zip(sources, held))]
    for load in loads:
        load.start()

    barrier = pltpu.get_barrier_semaphore()

    def greet_lane(k, _):
        pl.semaphore_signal(barrier, inc=1, device_id=(lax.rem(lane + k, lanes), node), device_id_type=MESH)
        return 0

    def greet_node(k, _):
        pl.semaphore_signal(barrier, inc=1, device_id=(lane, lax.rem(node + k, nodes)), device_id_type=MESH)
        return 0

    lax.fori_loop(1, lanes, greet_lane, 0)
    lax.fori_loop(1, nodes, greet_node, 0)

    for load in loads[:6]:
        load.wait()
    requests = request_ref[...].T
    for o in range(nodes):
        asked_out[o, :, 0:cap] = requests[o : o + 1, :]
    asked_in[pl.ds(node, 1), :, 0:cap] = asked_out[pl.ds(node, 1), :, 0:cap]
    lane_source[pl.ds(lane, 1)] = source_ref[...][None]
    lane_bucket[pl.ds(lane, 1)] = bucket_ref[...][None]
    te = frequency_ref.shape[1]
    frequency = jnp.broadcast_to(frequency_ref[...], (te, te)).T
    phase = jnp.broadcast_to(phase_ref[...], (te, te)).T
    ages = age_ref[...].astype(F32)
    for j in range(neighbours):
        enc[j] = cosine(frequency * ages[j : j + 1, :] + phase)
    node_row = lax.broadcasted_iota(jnp.int32, (owned, events), 0)
    own_member = (node_row == source_ref[...]).astype(F32)
    picker = own_member.T.astype(BF16)

    pl.semaphore_wait(barrier, lanes - 1 + nodes - 1)

    def lane_copies(k):
        to = lax.rem(lane + k, lanes)
        return [
            pltpu.make_async_remote_copy(
                src_ref=ref, dst_ref=held.at[lane], send_sem=lane_send.at[i, k], recv_sem=lane_recv.at[i, k],
                device_id=(to, node), device_id_type=MESH,
            )
            for i, (ref, held) in enumerate(((source_ref, lane_source), (bucket_ref, lane_bucket)))
        ]

    def ask_copy(k):
        to = lax.rem(node + k, nodes)
        return pltpu.make_async_remote_copy(
            src_ref=asked_out.at[to], dst_ref=asked_in.at[node], send_sem=ask_send.at[k], recv_sem=ask_recv.at[k],
            device_id=(lane, to), device_id_type=MESH,
        )

    def row_copy(k):
        to = lax.rem(node + k, nodes)
        return pltpu.make_async_remote_copy(
            src_ref=send_buf.at[to], dst_ref=far.at[node], send_sem=row_send.at[k], recv_sem=row_recv.at[k],
            device_id=(lane, to), device_id_type=MESH,
        )

    def loop(count, body):
        def step(k, _):
            body(k)
            return 0

        lax.fori_loop(1, count, step, 0)

    loop(lanes, lambda k: [copy.start() for copy in lane_copies(k)])
    loop(nodes, lambda k: ask_copy(k).start())
    loop(lanes, lambda k: [copy.wait() for copy in lane_copies(k)])

    for load in loads[6:11]:
        load.wait()
    ones = jnp.ones((te, events), BF16)
    sums = []
    for l in range(lanes):
        member = (node_row == lane_source[l]).astype(F32)
        encoded = cosine(frequency * lane_bucket[l].astype(F32) + phase)
        sums.append(nt(member, encoded, EXACT))
        touched[l] = nt(member.astype(BF16), ones)
    summed[...] = nn(jnp.concatenate(sums, axis=0), wm[...], EXACT).reshape(lanes, owned, channels)
    decay = -decay_ref[...]
    state = start_ref[...]

    def after(state, count, added):
        return jnp.exp(decay * jnp.concatenate([count] * (channels // te), axis=1)) * state + added

    for l in range(lanes - 1):
        state = jnp.where(l < lane, after(state, touched[l], summed[l]), state)
    memory_ref[...] = after(state, touched[pl.ds(lane, 1)][0], summed[pl.ds(lane, 1)][0])
    rows = state.astype(BF16)
    table_own[...] = rows

    loop(nodes, lambda k: ask_copy(k).wait())
    asked = jnp.concatenate([asked_in[o, :, :] for o in range(nodes)], axis=0).T
    node_lane = lax.broadcasted_iota(jnp.int32, (cap, owned), 1)
    picks = jnp.concatenate([(asked[0:cap, o : o + 1] == node_lane).astype(F32) for o in range(nodes)], axis=0)
    send_buf[...] = nn(picks.astype(BF16), rows).astype(BF16).reshape(nodes, cap, channels)
    loop(nodes, lambda k: row_copy(k).start())
    far[pl.ds(node, 1)] = send_buf[pl.ds(node, 1)]

    for load in loads[11:]:
        load.wait()
    query = nn(picker, nn(rows, wq[...]).astype(BF16)).astype(BF16)
    base_ref[...] = nn(nn(picker, rows).astype(BF16), ws[...])
    timed[...] = jnp.zeros_like(timed)
    for h in range(HEADS):
        head = query[:, h * size : (h + 1) * size]
        qk[h * events : (h + 1) * events, :] = nt(head, wkv[:, h * size : (h + 1) * size]).astype(BF16)
        spread = nt(wt[:, h * size : (h + 1) * size], head)
        for j in range(neighbours):
            timed[h, j : j + 1, :] = jnp.sum(spread * enc[j], axis=0, keepdims=True)
    value[total : total + owned, :] = nn(rows, wkv[:, width:]).astype(BF16)
    own_score = nt(rows, qk[...])
    scores[...] = jnp.zeros_like(scores)
    for h in range(HEADS):
        scores[h, neighbours : neighbours + 1, :] = jnp.sum(
            own_member * own_score[:, h * events : (h + 1) * events], axis=0, keepdims=True
        )
    acc[...] = jnp.zeros_like(acc)

    loop(nodes, lambda k: row_copy(k).wait())
    table = far[...].reshape(total, channels)
    value[0:total, :] = nn(table, wkv[:, width:]).astype(BF16)
    score[...] = nt(table, qk[...])

    piece = 32
    piece_row = lax.broadcasted_iota(jnp.int32, (piece, events), 0)

    def gather(c, _):
        base = pl.multiple_of(c * piece, piece)
        for j in range(neighbours):
            hit = (piece_row + base) == slot_ref[j : j + 1, :]
            for h in range(HEADS):
                found = jnp.where(hit, score[pl.ds(base, piece), h * events : (h + 1) * events], 0.0)
                acc[h, j] += jnp.sum(found.reshape(piece // 8, 8, events), axis=0)
        return 0

    lax.fori_loop(0, total // piece, gather, 0)
    for h in range(HEADS):
        for j in range(neighbours):
            scores[h, j : j + 1, :] = jnp.sum(acc[h, j], axis=0, keepdims=True)
    logits = (scores[...] + timed[...]) * (1.0 / math.sqrt(size))
    place = lax.broadcasted_iota(jnp.int32, logits.shape, 1)
    valid = (place < count_ref[...][None]) | (place == neighbours)
    logits = jnp.where(valid, logits, -1e30)
    expo = jnp.where(valid, jnp.exp(logits - jnp.max(logits, axis=1, keepdims=True)), 0.0)
    scores[...] = (expo / jnp.sum(expo, axis=1, keepdims=True)).astype(BF16).astype(F32)

    def scatter(c, _):
        base = pl.multiple_of(c * piece, piece)
        hits = [(piece_row + base) == slot_ref[j : j + 1, :] for j in range(neighbours)]
        for h in range(HEADS):
            put = jnp.zeros((piece, events), F32)
            for j in range(neighbours):
                put += jnp.where(hits[j], scores[h, j : j + 1, :], 0.0)
            mix[pl.ds(base, piece), h * events : (h + 1) * events] = put.astype(BF16)
        return 0

    lax.fori_loop(0, total // piece, scatter, 0)
    for h in range(HEADS):
        mix[total : total + owned, h * events : (h + 1) * events] = (
            own_member * scores[h, neighbours : neighbours + 1, :]
        ).astype(BF16)
        attended_ref[:, h * size : (h + 1) * size] = tn(
            mix[:, h * events : (h + 1) * events], value[:, h * size : (h + 1) * size]
        ).astype(BF16)


def finish(
    attended_hbm, base_hbm, memory_hbm, output_hbm, embedding_ref, lane_memory_ref, attended_ref, base_ref, output_ref, sem
):
    half = output_ref.shape[0] // 2
    loads = [
        pltpu.make_async_copy(a, b, sem.at[i])
        for i, (a, b) in enumerate(
            (
                (attended_hbm, attended_ref), (output_hbm.at[0:half], output_ref.at[0:half]), (base_hbm, base_ref),
                (output_hbm.at[half:], output_ref.at[half:]), (memory_hbm, lane_memory_ref),
            )
        )
    ]
    for load in loads:
        load.start()
    for load in loads[0:3]:
        load.wait()
    part = nn(attended_ref[:, 0:half], output_ref[0:half, :]) + base_ref[...]
    loads[3].wait()
    embedding_ref[...] = (nn(attended_ref[:, half:], output_ref[half:, :]) + part).astype(BF16)
    loads[4].wait()


def local(
    source_row, time_bucket, neighbour_slot, neighbour_age, neighbour_count, request_rows, memory_start, decay_rate,
    time_frequency, time_phase, weight_message, weight_query, weight_keyval, weight_time, weight_output, weight_skip,
):
    lanes, nodes = lax.axis_size("lane"), lax.axis_size("node")
    owned, channels = memory_start.shape
    events, neighbours = neighbour_slot.shape
    cap = request_rows.shape[1]
    te, width = weight_time.shape
    total = nodes * cap
    row = lambda x: x.reshape(1, -1)
    vmem = pl.BlockSpec(memory_space=pltpu.VMEM)
    hbm = pl.BlockSpec(memory_space=pltpu.HBM)
    dma = pltpu.SemaphoreType.DMA
    attended, base, memory = pl.pallas_call(
        functools.partial(kernel, lanes, nodes),
        out_shape=(
            jax.ShapeDtypeStruct((events, width), BF16),
            jax.ShapeDtypeStruct((events, width), F32),
            jax.ShapeDtypeStruct((owned, channels), F32),
        ),
        in_specs=[hbm] * 15,
        out_specs=(vmem, vmem, vmem),
        scratch_shapes=[
            pltpu.VMEM((1, events), jnp.int32),
            pltpu.VMEM((1, events), jnp.int32),
            pltpu.VMEM((cap, nodes), jnp.int32),
            pltpu.VMEM((1, te), F32),
            pltpu.VMEM((1, te), F32),
            pltpu.VMEM((neighbours, events), jnp.int32),
            pltpu.VMEM((neighbours, events), jnp.int32),
            pltpu.VMEM((1, events), jnp.int32),
            pltpu.VMEM((1, channels), F32),
            pltpu.VMEM((owned, channels), F32),
            pltpu.VMEM(weight_message.shape, F32),
            pltpu.VMEM(weight_query.shape, BF16),
            pltpu.VMEM(weight_keyval.shape, BF16),
            pltpu.VMEM(weight_time.shape, BF16),
            pltpu.VMEM(weight_skip.shape, BF16),
            dma((15,)),
            pltpu.VMEM((lanes, 1, events), jnp.int32),
            pltpu.VMEM((lanes, 1, events), jnp.int32),
            pltpu.VMEM((nodes, 1, 128), jnp.int32),
            pltpu.VMEM((nodes, 1, 128), jnp.int32),
            pltpu.VMEM((nodes, cap, channels), BF16),
            pltpu.VMEM((nodes, cap, channels), BF16),
            pltpu.VMEM((lanes, owned, channels), F32),
            pltpu.VMEM((lanes, owned, te), F32),
            pltpu.VMEM((neighbours, te, events), F32),
            pltpu.VMEM((HEADS, 16, events), F32),
            pltpu.VMEM((HEADS, neighbours, 8, events), F32),
            pltpu.VMEM((HEADS, 16, events), F32),
            pltpu.VMEM((owned, channels), BF16),
            pltpu.VMEM((total + owned, width), BF16),
            pltpu.VMEM((total, HEADS * events), F32),
            pltpu.VMEM((total + owned, HEADS * events), BF16),
            pltpu.VMEM((HEADS * events, channels), BF16),
            dma((2, lanes)),
            dma((2, lanes)),
            dma((nodes,)),
            dma((nodes,)),
            dma((nodes,)),
            dma((nodes,)),
        ],
        compiler_params=pltpu.CompilerParams(
            collective_id=0, has_side_effects=True, vmem_limit_bytes=56 * 1024 * 1024
        ),
    )(
        row(source_row), row(time_bucket), request_rows.T, row(time_frequency), row(time_phase), neighbour_age.T,
        neighbour_slot.T, row(neighbour_count), row(decay_rate), memory_start, weight_message, weight_query,
        weight_keyval, weight_time, weight_skip,
    )
    embedding, memory = pl.pallas_call(
        finish,
        out_shape=(
            jax.ShapeDtypeStruct((events, width), BF16),
            jax.ShapeDtypeStruct((owned, channels), F32),
        ),
        in_specs=[hbm] * 4,
        out_specs=(vmem, vmem),
        scratch_shapes=[
            pltpu.VMEM((events, width), BF16),
            pltpu.VMEM((events, width), F32),
            pltpu.VMEM(weight_output.shape, BF16),
            dma((5,)),
        ],
        compiler_params=pltpu.CompilerParams(vmem_limit_bytes=56 * 1024 * 1024),
    )(attended, base, memory, weight_output)
    return embedding, memory[None]


def solution(mesh):
    both, rows = P(("lane", "node")), P(("lane", "node"), None)
    return jax.shard_map(
        local,
        mesh=mesh,
        in_specs=(both, both, rows, rows, both, rows, P("node", None)) + (P(),) * 9,
        out_specs=(rows, P("lane", "node", None)),
        check_vma=False,
    )
```

```python
import functools
import math

import jax
import jax.numpy as jnp
from jax import lax
from jax.experimental import pallas as pl
from jax.experimental.pallas import tpu as pltpu
from jax.sharding import PartitionSpec as P

MESH = pl.DeviceIdType.MESH
HEADS = 8
RING = 8
F32, BF16 = jnp.float32, jnp.bfloat16
EXACT = lax.Precision.HIGHEST
SINE = (0.5, -0.020833322778344154, 0.0002604078035801649, -1.5475785630769678e-06, 5.088033105948853e-09)
TURN_HIGH = 6.28125
TURN_LOW = 2.0 * math.pi - TURN_HIGH
ROUNDER = 12582912.0


def cosine(angle):
    turns = (angle * (0.5 / math.pi) + ROUNDER) - ROUNDER
    rest = (angle - turns * TURN_HIGH) - turns * TURN_LOW
    square = rest * rest
    poly = SINE[4]
    for term in SINE[3::-1]:
        poly = poly * square + term
    half = rest * poly
    return 1.0 - 2.0 * (half * half)


def nn(a, b, precision=None):
    return lax.dot_general(a, b, (((1,), (0,)), ((), ())), precision=precision, preferred_element_type=F32)


def nt(a, b, precision=None):
    return lax.dot_general(a, b, (((1,), (1,)), ((), ())), precision=precision, preferred_element_type=F32)


def tn(a, b):
    return lax.dot_general(a, b, (((0,), (0,)), ((), ())), preferred_element_type=F32)


def kernel(
    lanes, nodes,
    source_hbm, bucket_hbm, request_hbm, frequency_hbm, phase_hbm, age_hbm, slot_hbm, count_hbm, decay_hbm, start_hbm,
    message_hbm, query_hbm, keyval_hbm, time_hbm, skip_hbm,
    attended_ref, base_ref, memory_ref,
    event_ref, request_ref, frequency_ref, phase_ref, age_ref, slot_ref, count_ref, decay_ref, start_ref,
    wm, wq, wkv, wt, ws, load_sem,
    lane_event, asked_out, asked_in, send_buf, far,
    summed, touched, enc, timed, acc, scores, table_own, value, score, mix, qk,
    lane_send, lane_recv, ask_send, ask_recv, row_send, row_recv, met,
):
    lane, node = lax.axis_index("lane"), lax.axis_index("node")
    owned, channels = start_ref.shape
    neighbours, events = slot_ref.shape
    cap = request_ref.shape[0]
    width = wq.shape[1]
    size = width // HEADS
    total = nodes * cap
    shift = cap.bit_length() - 1

    sources = (
        source_hbm, bucket_hbm, request_hbm, frequency_hbm, phase_hbm, age_hbm, slot_hbm, count_hbm, decay_hbm,
        start_hbm, message_hbm, query_hbm, keyval_hbm, time_hbm, skip_hbm,
    )
    held = (
        event_ref.at[0:1], event_ref.at[1:2], request_ref, frequency_ref, phase_ref, age_ref, slot_ref, count_ref, decay_ref,
        start_ref, wm, wq, wkv, wt, ws,
    )
    loads = [pltpu.make_async_copy(a, b, load_sem.at[i]) for i, (a, b) in enumerate(zip(sources, held))]

    barrier = pltpu.get_barrier_semaphore()
    groups = nodes // RING
    group, place = node // RING, lax.rem(node, RING)

    def greet_lane(k, _):
        pl.semaphore_signal(barrier, inc=1, device_id=(lax.rem(lane + k, lanes), node), device_id_type=MESH)
        return 0

    def greet_ring(k, _):
        to = group * RING + lax.rem(place + k, RING)
        pl.semaphore_signal(barrier, inc=1, device_id=(lane, to), device_id_type=MESH)
        return 0

    def greet_group(semaphore):
        def greet(k, _):
            to = lax.rem(group + k, groups) * RING + place
            pl.semaphore_signal(semaphore, inc=1, device_id=(lane, to), device_id_type=MESH)
            return 0

        lax.fori_loop(1, groups, greet, 0)

    lax.fori_loop(1, RING, greet_ring, 0)
    greet_group(barrier)
    lax.fori_loop(1, lanes, greet_lane, 0)
    for load in loads:
        load.start()

    for load in loads[:6]:
        load.wait()
    requests = request_ref[...].T
    for o in range(nodes):
        asked_out[o, :, 0:cap] = requests[o : o + 1, :]
    asked_in[pl.ds(node, 1), :, 0:cap] = asked_out[pl.ds(node, 1), :, 0:cap]
    lane_event[pl.ds(lane, 1)] = event_ref[...][None]
    te = frequency_ref.shape[1]
    frequency = jnp.broadcast_to(frequency_ref[...], (te, te)).T
    phase = jnp.broadcast_to(phase_ref[...], (te, te)).T
    ages = age_ref[...].astype(F32)
    for j in range(neighbours):
        enc[j] = cosine(frequency * ages[j : j + 1, :] + phase)
    node_row = lax.broadcasted_iota(jnp.int32, (owned, events), 0)
    own_member = (node_row == event_ref[0:1, :]).astype(F32)
    picker = own_member.T.astype(BF16)

    pl.semaphore_wait(barrier, lanes - 1 + RING - 1 + groups - 1)

    def lane_copy(k):
        to = lax.rem(lane + k, lanes)
        return pltpu.make_async_remote_copy(
            src_ref=event_ref, dst_ref=lane_event.at[lane], send_sem=lane_send.at[k], recv_sem=lane_recv.at[k],
            device_id=(to, node), device_id_type=MESH,
        )

    def ask_copy(k):
        to = lax.rem(node + k, nodes)
        return pltpu.make_async_remote_copy(
            src_ref=asked_out.at[to], dst_ref=asked_in.at[node], send_sem=ask_send.at[k], recv_sem=ask_recv.at[k],
            device_id=(lane, to), device_id_type=MESH,
        )

    def row_copy(k):
        to = lax.rem(node + k, nodes)
        return pltpu.make_async_remote_copy(
            src_ref=send_buf.at[to], dst_ref=far.at[k], send_sem=row_send.at[k], recv_sem=row_recv.at[k],
            device_id=(lane, to), device_id_type=MESH,
        )

    def loop(count, body):
        def step(k, _):
            body(k)
            return 0

        lax.fori_loop(1, count, step, 0)

    def wait_row(k, _):
        row_copy(k).wait()
        return 0

    loop(lanes, lambda k: lane_copy(k).start())
    greet_group(met)
    pl.semaphore_wait(met, groups - 1)
    loop(nodes, lambda k: ask_copy(k).start())
    loop(lanes, lambda k: lane_copy(k).wait())

    for load in loads[6:11]:
        load.wait()
    ones = jnp.ones((te, events), BF16)
    sums = []
    for l in range(lanes):
        member = (node_row == lane_event[l, 0:1, :]).astype(F32)
        encoded = cosine(frequency * lane_event[l, 1:2, :].astype(F32) + phase)
        sums.append(nt(member, encoded, EXACT))
        touched[l] = nt(member.astype(BF16), ones)
    summed[...] = nn(jnp.concatenate(sums, axis=0), wm[...], EXACT).reshape(lanes, owned, channels)
    decay = -decay_ref[...]
    state = start_ref[...]

    def after(state, count, added):
        return jnp.exp(decay * jnp.concatenate([count] * (channels // te), axis=1)) * state + added

    for l in range(lanes - 1):
        state = jnp.where(l < lane, after(state, touched[l], summed[l]), state)
    memory_ref[...] = after(state, touched[pl.ds(lane, 1)][0], summed[pl.ds(lane, 1)][0])
    rows = state.astype(BF16)
    table_own[...] = rows

    loop(nodes, lambda k: ask_copy(k).wait())
    asked = jnp.concatenate([asked_in[o, :, :] for o in range(nodes)], axis=0).T
    node_lane = lax.broadcasted_iota(jnp.int32, (cap, owned), 1)
    picks = jnp.concatenate([(asked[0:cap, o : o + 1] == node_lane).astype(F32) for o in range(nodes)], axis=0)
    send_buf[...] = nn(picks.astype(BF16), rows).astype(BF16).reshape(nodes, cap, channels)
    loop(nodes, lambda k: row_copy(k).start())
    far[0:1] = send_buf[pl.ds(node, 1)]

    for load in loads[11:]:
        load.wait()
    query = nn(picker, nn(rows, wq[...]).astype(BF16)).astype(BF16)
    base_ref[...] = nn(nn(picker, rows).astype(BF16), ws[...])
    timed[...] = jnp.zeros_like(timed)
    for h in range(HEADS):
        head = query[:, h * size : (h + 1) * size]
        qk[h * events : (h + 1) * events, :] = nt(head, wkv[:, h * size : (h + 1) * size]).astype(BF16)
        spread = nt(wt[:, h * size : (h + 1) * size], head)
        for j in range(neighbours):
            timed[h, j : j + 1, :] = jnp.sum(spread * enc[j], axis=0, keepdims=True)
    value[total : total + owned, :] = nn(rows, wkv[:, width:]).astype(BF16)
    own_score = nt(rows, qk[...])
    scores[...] = jnp.zeros_like(scores)
    for h in range(HEADS):
        scores[h, neighbours : neighbours + 1, :] = jnp.sum(
            own_member * own_score[:, h * events : (h + 1) * events], axis=0, keepdims=True
        )
    acc[...] = jnp.zeros_like(acc)

    distance = node - lax.shift_right_logical(slot_ref[...], shift)
    distance = jnp.where(distance < 0, distance + nodes, distance)
    slot_ref[...] = distance * cap + (slot_ref[...] & (cap - 1))

    piece = 32
    part = RING * cap
    piece_row = lax.broadcasted_iota(jnp.int32, (piece, events), 0)

    for c in range(nodes // RING):
        lax.fori_loop(max(1, c * RING), (c + 1) * RING, wait_row, 0)
        table = far[c * RING : (c + 1) * RING].reshape(part, channels)
        score[...] = nt(table, qk[...])

        def gather(p, _, c=c):
            base = pl.multiple_of(p * piece, piece)
            for j in range(neighbours):
                hit = (piece_row + (base + c * part)) == slot_ref[j : j + 1, :]
                for h in range(HEADS):
                    found = jnp.where(hit, score[pl.ds(base, piece), h * events : (h + 1) * events], 0.0)
                    acc[h, j] += jnp.sum(found.reshape(piece // 8, 8, events), axis=0)
            return 0

        lax.fori_loop(0, part // piece, gather, 0)
        value[c * part : (c + 1) * part, :] = nn(table, wkv[:, width:]).astype(BF16)
    for h in range(HEADS):
        for j in range(neighbours):
            scores[h, j : j + 1, :] = jnp.sum(acc[h, j], axis=0, keepdims=True)
    logits = (scores[...] + timed[...]) * (1.0 / math.sqrt(size))
    order = lax.broadcasted_iota(jnp.int32, logits.shape, 1)
    valid = (order < count_ref[...][None]) | (order == neighbours)
    logits = jnp.where(valid, logits, -1e30)
    expo = jnp.where(valid, jnp.exp(logits - jnp.max(logits, axis=1, keepdims=True)), 0.0)
    scores[...] = (expo / jnp.sum(expo, axis=1, keepdims=True)).astype(BF16).astype(F32)

    def scatter(c, _):
        base = pl.multiple_of(c * piece, piece)
        hits = [(piece_row + base) == slot_ref[j : j + 1, :] for j in range(neighbours)]
        for h in range(HEADS):
            put = jnp.zeros((piece, events), F32)
            for j in range(neighbours):
                put += jnp.where(hits[j], scores[h, j : j + 1, :], 0.0)
            mix[pl.ds(base, piece), h * events : (h + 1) * events] = put.astype(BF16)
        return 0

    lax.fori_loop(0, total // piece, scatter, 0)
    for h in range(HEADS):
        mix[total : total + owned, h * events : (h + 1) * events] = (
            own_member * scores[h, neighbours : neighbours + 1, :]
        ).astype(BF16)
        attended_ref[:, h * size : (h + 1) * size] = tn(
            mix[:, h * events : (h + 1) * events], value[:, h * size : (h + 1) * size]
        ).astype(BF16)


def finish(
    attended_hbm, base_hbm, memory_hbm, output_hbm, embedding_ref, lane_memory_ref, attended_ref, base_ref, output_ref, sem
):
    half = output_ref.shape[0] // 2
    loads = [
        pltpu.make_async_copy(a, b, sem.at[i])
        for i, (a, b) in enumerate(
            (
                (attended_hbm, attended_ref), (output_hbm.at[0:half], output_ref.at[0:half]), (base_hbm, base_ref),
                (output_hbm.at[half:], output_ref.at[half:]), (memory_hbm, lane_memory_ref),
            )
        )
    ]
    for load in loads:
        load.start()
    for load in loads[0:3]:
        load.wait()
    part = nn(attended_ref[:, 0:half], output_ref[0:half, :]) + base_ref[...]
    loads[3].wait()
    embedding_ref[...] = (nn(attended_ref[:, half:], output_ref[half:, :]) + part).astype(BF16)
    loads[4].wait()


def local(
    source_row, time_bucket, neighbour_slot, neighbour_age, neighbour_count, request_rows, memory_start, decay_rate,
    time_frequency, time_phase, weight_message, weight_query, weight_keyval, weight_time, weight_output, weight_skip,
):
    lanes, nodes = lax.axis_size("lane"), lax.axis_size("node")
    owned, channels = memory_start.shape
    events, neighbours = neighbour_slot.shape
    cap = request_rows.shape[1]
    te, width = weight_time.shape
    total = nodes * cap
    row = lambda x: x.reshape(1, -1)
    vmem = pl.BlockSpec(memory_space=pltpu.VMEM)
    hbm = pl.BlockSpec(memory_space=pltpu.HBM)
    dma = pltpu.SemaphoreType.DMA
    attended, base, memory = pl.pallas_call(
        functools.partial(kernel, lanes, nodes),
        out_shape=(
            jax.ShapeDtypeStruct((events, width), BF16),
            jax.ShapeDtypeStruct((events, width), F32),
            jax.ShapeDtypeStruct((owned, channels), F32),
        ),
        in_specs=[hbm] * 15,
        out_specs=(vmem, vmem, vmem),
        scratch_shapes=[
            pltpu.VMEM((2, events), jnp.int32),
            pltpu.VMEM((cap, nodes), jnp.int32),
            pltpu.VMEM((1, te), F32),
            pltpu.VMEM((1, te), F32),
            pltpu.VMEM((neighbours, events), jnp.int32),
            pltpu.VMEM((neighbours, events), jnp.int32),
            pltpu.VMEM((1, events), jnp.int32),
            pltpu.VMEM((1, channels), F32),
            pltpu.VMEM((owned, channels), F32),
            pltpu.VMEM(weight_message.shape, F32),
            pltpu.VMEM(weight_query.shape, BF16),
            pltpu.VMEM(weight_keyval.shape, BF16),
            pltpu.VMEM(weight_time.shape, BF16),
            pltpu.VMEM(weight_skip.shape, BF16),
            dma((15,)),
            pltpu.VMEM((lanes, 2, events), jnp.int32),
            pltpu.VMEM((nodes, 1, 128), jnp.int32),
            pltpu.VMEM((nodes, 1, 128), jnp.int32),
            pltpu.VMEM((nodes, cap, channels), BF16),
            pltpu.VMEM((nodes, cap, channels), BF16),
            pltpu.VMEM((lanes, owned, channels), F32),
            pltpu.VMEM((lanes, owned, te), F32),
            pltpu.VMEM((neighbours, te, events), F32),
            pltpu.VMEM((HEADS, 16, events), F32),
            pltpu.VMEM((HEADS, neighbours, 8, events), F32),
            pltpu.VMEM((HEADS, 16, events), F32),
            pltpu.VMEM((owned, channels), BF16),
            pltpu.VMEM((total + owned, width), BF16),
            pltpu.VMEM((RING * cap, HEADS * events), F32),
            pltpu.VMEM((total + owned, HEADS * events), BF16),
            pltpu.VMEM((HEADS * events, channels), BF16),
            dma((lanes,)),
            dma((lanes,)),
            dma((nodes,)),
            dma((nodes,)),
            dma((nodes,)),
            dma((nodes,)),
            pltpu.SemaphoreType.REGULAR,
        ],
        compiler_params=pltpu.CompilerParams(
            collective_id=0, has_side_effects=True, vmem_limit_bytes=56 * 1024 * 1024
        ),
    )(
        row(source_row), row(time_bucket), request_rows.T, row(time_frequency), row(time_phase), neighbour_age.T,
        neighbour_slot.T, row(neighbour_count), row(decay_rate), memory_start, weight_message, weight_query,
        weight_keyval, weight_time, weight_skip,
    )
    embedding, memory = pl.pallas_call(
        finish,
        out_shape=(
            jax.ShapeDtypeStruct((events, width), BF16),
            jax.ShapeDtypeStruct((owned, channels), F32),
        ),
        in_specs=[hbm] * 4,
        out_specs=(vmem, vmem),
        scratch_shapes=[
            pltpu.VMEM((events, width), BF16),
            pltpu.VMEM((events, width), F32),
            pltpu.VMEM(weight_output.shape, BF16),
            dma((5,)),
        ],
        compiler_params=pltpu.CompilerParams(vmem_limit_bytes=56 * 1024 * 1024),
    )(attended, base, memory, weight_output)
    return embedding, memory[None]


def solution(mesh):
    both, rows = P(("lane", "node")), P(("lane", "node"), None)
    return jax.shard_map(
        local,
        mesh=mesh,
        in_specs=(both, both, rows, rows, both, rows, P("node", None)) + (P(),) * 9,
        out_specs=(rows, P("lane", "node", None)),
        check_vma=False,
    )
```

```python
import functools
import math

import jax
import jax.numpy as jnp
from jax import lax
from jax.experimental import pallas as pl
from jax.experimental.pallas import tpu as pltpu
from jax.sharding import PartitionSpec as P

MESH = pl.DeviceIdType.MESH
HEADS = 8
RING = 8
F32, BF16 = jnp.float32, jnp.bfloat16
SINE = (0.5, -0.020833322778344154, 0.0002604078035801649, -1.5475785630769678e-06, 5.088033105948853e-09)
TURN_HIGH = 6.28125
TURN_LOW = 2.0 * math.pi - TURN_HIGH
ROUNDER = 12582912.0


def cosine(angle):
    turns = (angle * (0.5 / math.pi) + ROUNDER) - ROUNDER
    rest = (angle - turns * TURN_HIGH) - turns * TURN_LOW
    square = rest * rest
    poly = SINE[4]
    for term in SINE[3::-1]:
        poly = poly * square + term
    half = rest * poly
    return 1.0 - 2.0 * (half * half)


def nn(a, b):
    return lax.dot_general(a, b, (((1,), (0,)), ((), ())), preferred_element_type=F32)


def nt(a, b):
    return lax.dot_general(a, b, (((1,), (1,)), ((), ())), preferred_element_type=F32)


def tn(a, b):
    return lax.dot_general(a, b, (((0,), (0,)), ((), ())), preferred_element_type=F32)


def kernel(
    lanes, nodes,
    source_hbm, bucket_hbm, request_hbm, frequency_hbm, phase_hbm, age_hbm, slot_hbm, count_hbm, decay_hbm, start_hbm,
    message_hbm, query_hbm, keyval_hbm, time_hbm, skip_hbm,
    attended_ref, base_ref, memory_ref,
    event_ref, request_ref, frequency_ref, phase_ref, age_ref, slot_ref, count_ref, decay_ref, start_ref,
    wm, wq, wkv, wt, ws, load_sem,
    lane_event, asked_out, asked_in, send_buf, far,
    summed, touched, enc, timed, acc, scores, table_own, value, score, mix, qk,
    lane_send, lane_recv, ask_send, ask_recv, row_send, row_recv, met,
):
    lane, node = lax.axis_index("lane"), lax.axis_index("node")
    owned, channels = start_ref.shape
    neighbours, events = slot_ref.shape
    cap = request_ref.shape[0]
    width = wq.shape[1]
    size = width // HEADS
    total = nodes * cap
    shift = cap.bit_length() - 1

    sources = (
        source_hbm, bucket_hbm, request_hbm, frequency_hbm, phase_hbm, age_hbm, slot_hbm, count_hbm, decay_hbm,
        start_hbm, message_hbm, query_hbm, keyval_hbm, time_hbm, skip_hbm,
    )
    held = (
        event_ref.at[0:1], event_ref.at[1:2], request_ref, frequency_ref, phase_ref, age_ref, slot_ref, count_ref, decay_ref,
        start_ref, wm, wq, wkv, wt, ws,
    )
    loads = [pltpu.make_async_copy(a, b, load_sem.at[i]) for i, (a, b) in enumerate(zip(sources, held))]

    barrier = pltpu.get_barrier_semaphore()
    groups = nodes // RING
    group, place = node // RING, lax.rem(node, RING)

    def greet_lane(k, _):
        pl.semaphore_signal(barrier, inc=1, device_id=(lax.rem(lane + k, lanes), node), device_id_type=MESH)
        return 0

    def greet_ring(k, _):
        to = group * RING + lax.rem(place + k, RING)
        pl.semaphore_signal(barrier, inc=1, device_id=(lane, to), device_id_type=MESH)
        return 0

    def greet_group(semaphore):
        def greet(k, _):
            to = lax.rem(group + k, groups) * RING + place
            pl.semaphore_signal(semaphore, inc=1, device_id=(lane, to), device_id_type=MESH)
            return 0

        lax.fori_loop(1, groups, greet, 0)

    lax.fori_loop(1, RING, greet_ring, 0)
    greet_group(barrier)
    lax.fori_loop(1, lanes, greet_lane, 0)
    for load in loads:
        load.start()

    for load in loads[:6]:
        load.wait()
    requests = request_ref[...].T
    for o in range(nodes):
        asked_out[o, :, 0:cap] = requests[o : o + 1, :]
    asked_in[0:1, :, 0:cap] = asked_out[pl.ds(node, 1), :, 0:cap]
    lane_event[pl.ds(lane, 1)] = event_ref[...][None]
    te = frequency_ref.shape[1]
    frequency = jnp.broadcast_to(frequency_ref[...], (te, te)).T
    phase = jnp.broadcast_to(phase_ref[...], (te, te)).T
    ages = age_ref[...].astype(F32)
    for j in range(neighbours):
        enc[j] = cosine(frequency * ages[j : j + 1, :] + phase)
    node_row = lax.broadcasted_iota(jnp.int32, (owned, events), 0)
    own_member = (node_row == event_ref[0:1, :]).astype(F32)
    picker = own_member.T.astype(BF16)

    pl.semaphore_wait(barrier, lanes - 1 + RING - 1 + groups - 1)

    def lane_copy(k):
        to = lax.rem(lane + k, lanes)
        return pltpu.make_async_remote_copy(
            src_ref=event_ref, dst_ref=lane_event.at[lane], send_sem=lane_send.at[k], recv_sem=lane_recv.at[k],
            device_id=(to, node), device_id_type=MESH,
        )

    def ask_copy(k):
        to = lax.rem(node + k, nodes)
        return pltpu.make_async_remote_copy(
            src_ref=asked_out.at[to], dst_ref=asked_in.at[k], send_sem=ask_send.at[k], recv_sem=ask_recv.at[k],
            device_id=(lane, to), device_id_type=MESH,
        )

    def row_copy(k):
        to = lax.rem(node + nodes - k, nodes)
        return pltpu.make_async_remote_copy(
            src_ref=send_buf.at[k], dst_ref=far.at[k], send_sem=row_send.at[k], recv_sem=row_recv.at[k],
            device_id=(lane, to), device_id_type=MESH,
        )

    def loop(count, body):
        def step(k, _):
            body(k)
            return 0

        lax.fori_loop(1, count, step, 0)

    def wait_row(k, _):
        row_copy(k).wait_recv()
        return 0

    def start_row(k, _):
        row_copy(k).start()
        return 0

    def wait_ask(k, _):
        ask_copy(k).wait_recv()
        return 0

    def sent(k):
        ask_copy(k).wait_send()
        row_copy(k).wait_send()

    loop(lanes, lambda k: lane_copy(k).start())
    greet_group(met)
    pl.semaphore_wait(met, groups - 1)
    loop(nodes, lambda k: ask_copy(k).start())
    loop(lanes, lambda k: lane_copy(k).wait())

    for load in loads[6:11]:
        load.wait()
    ones = jnp.ones((te, events), BF16)
    sums = []
    for l in range(lanes):
        member = (node_row == lane_event[l, 0:1, :]).astype(F32).astype(BF16)
        encoded = cosine(frequency * lane_event[l, 1:2, :].astype(F32) + phase)
        sums.append(nt(member, encoded.astype(BF16)))
        touched[l] = nt(member, ones)
    summed[...] = nn(jnp.concatenate(sums, axis=0).astype(BF16), wm[...].astype(BF16)).reshape(lanes, owned, channels)
    decay = -decay_ref[...]
    state = start_ref[...]

    def after(state, count, added):
        return jnp.exp(decay * jnp.concatenate([count] * (channels // te), axis=1)) * state + added

    for l in range(lanes - 1):
        state = jnp.where(l < lane, after(state, touched[l], summed[l]), state)
    memory_ref[...] = after(state, touched[pl.ds(lane, 1)][0], summed[pl.ds(lane, 1)][0])
    rows = state.astype(BF16)
    table_own[...] = rows

    node_lane = lax.broadcasted_iota(jnp.int32, (cap, owned), 1)
    for c in range(nodes // RING):
        near, past = c * RING, (c + 1) * RING
        lax.fori_loop(max(1, near), past, wait_ask, 0)
        asked = jnp.concatenate([asked_in[o, :, :] for o in range(near, past)], axis=0).T
        picks = jnp.concatenate([(asked[0:cap, o : o + 1] == node_lane).astype(F32) for o in range(RING)], axis=0)
        send_buf[near:past] = nn(picks.astype(BF16), rows).astype(BF16).reshape(RING, cap, channels)
        lax.fori_loop(max(1, near), past, start_row, 0)
    far[0:1] = send_buf[0:1]

    for load in loads[11:]:
        load.wait()
    query = nn(picker, nn(rows, wq[...]).astype(BF16)).astype(BF16)
    base_ref[...] = nn(nn(picker, rows).astype(BF16), ws[...])
    timed[...] = jnp.zeros_like(timed)
    for h in range(HEADS):
        head = query[:, h * size : (h + 1) * size]
        qk[h * events : (h + 1) * events, :] = nt(head, wkv[:, h * size : (h + 1) * size]).astype(BF16)
        spread = nt(wt[:, h * size : (h + 1) * size], head)
        for j in range(neighbours):
            timed[h, j : j + 1, :] = jnp.sum(spread * enc[j], axis=0, keepdims=True)
    value[total : total + owned, :] = nn(rows, wkv[:, width:]).astype(BF16)
    own_score = nt(rows, qk[...])
    scores[...] = jnp.zeros_like(scores)
    for h in range(HEADS):
        scores[h, neighbours : neighbours + 1, :] = jnp.sum(
            own_member * own_score[:, h * events : (h + 1) * events], axis=0, keepdims=True
        )
    acc[...] = jnp.zeros_like(acc)

    distance = lax.shift_right_logical(slot_ref[...], shift) - node
    distance = jnp.where(distance < 0, distance + nodes, distance)
    slot_ref[...] = distance * cap + (slot_ref[...] & (cap - 1))

    piece = 32
    part = RING * cap
    piece_row = lax.broadcasted_iota(jnp.int32, (piece, events), 0)

    for c in range(nodes // RING):
        lax.fori_loop(max(1, c * RING), (c + 1) * RING, wait_row, 0)
        table = far[c * RING : (c + 1) * RING].reshape(part, channels)
        score[...] = nt(table, qk[...])

        def gather(p, _, c=c):
            base = pl.multiple_of(p * piece, piece)
            for j in range(neighbours):
                hit = (piece_row + (base + c * part)) == slot_ref[j : j + 1, :]
                for h in range(HEADS):
                    found = jnp.where(hit, score[pl.ds(base, piece), h * events : (h + 1) * events], 0.0)
                    acc[h, j] += jnp.sum(found.reshape(piece // 8, 8, events), axis=0)
            return 0

        lax.fori_loop(0, part // piece, gather, 0)
        value[c * part : (c + 1) * part, :] = nn(table, wkv[:, width:]).astype(BF16)
    loop(nodes, sent)
    for h in range(HEADS):
        for j in range(neighbours):
            scores[h, j : j + 1, :] = jnp.sum(acc[h, j], axis=0, keepdims=True)
    logits = (scores[...] + timed[...]) * (1.0 / math.sqrt(size))
    order = lax.broadcasted_iota(jnp.int32, logits.shape, 1)
    valid = (order < count_ref[...][None]) | (order == neighbours)
    logits = jnp.where(valid, logits, -1e30)
    expo = jnp.where(valid, jnp.exp(logits - jnp.max(logits, axis=1, keepdims=True)), 0.0)
    scores[...] = (expo / jnp.sum(expo, axis=1, keepdims=True)).astype(BF16).astype(F32)

    def scatter(c, _):
        base = pl.multiple_of(c * piece, piece)
        hits = [(piece_row + base) == slot_ref[j : j + 1, :] for j in range(neighbours)]
        for h in range(HEADS):
            put = jnp.zeros((piece, events), F32)
            for j in range(neighbours):
                put += jnp.where(hits[j], scores[h, j : j + 1, :], 0.0)
            mix[pl.ds(base, piece), h * events : (h + 1) * events] = put.astype(BF16)
        return 0

    lax.fori_loop(0, total // piece, scatter, 0)
    for h in range(HEADS):
        mix[total : total + owned, h * events : (h + 1) * events] = (
            own_member * scores[h, neighbours : neighbours + 1, :]
        ).astype(BF16)
        attended_ref[:, h * size : (h + 1) * size] = tn(
            mix[:, h * events : (h + 1) * events], value[:, h * size : (h + 1) * size]
        ).astype(BF16)


def finish(
    attended_hbm, base_hbm, memory_hbm, output_hbm, embedding_ref, lane_memory_ref, attended_ref, base_ref, output_ref, sem
):
    half = output_ref.shape[0] // 2
    loads = [
        pltpu.make_async_copy(a, b, sem.at[i])
        for i, (a, b) in enumerate(
            (
                (attended_hbm, attended_ref), (output_hbm.at[0:half], output_ref.at[0:half]), (base_hbm, base_ref),
                (output_hbm.at[half:], output_ref.at[half:]), (memory_hbm, lane_memory_ref),
            )
        )
    ]
    for load in loads:
        load.start()
    for load in loads[0:3]:
        load.wait()
    part = nn(attended_ref[:, 0:half], output_ref[0:half, :]) + base_ref[...]
    loads[3].wait()
    embedding_ref[...] = (nn(attended_ref[:, half:], output_ref[half:, :]) + part).astype(BF16)
    loads[4].wait()


def local(
    source_row, time_bucket, neighbour_slot, neighbour_age, neighbour_count, request_rows, memory_start, decay_rate,
    time_frequency, time_phase, weight_message, weight_query, weight_keyval, weight_time, weight_output, weight_skip,
):
    lanes, nodes = lax.axis_size("lane"), lax.axis_size("node")
    owned, channels = memory_start.shape
    events, neighbours = neighbour_slot.shape
    cap = request_rows.shape[1]
    te, width = weight_time.shape
    total = nodes * cap
    row = lambda x: x.reshape(1, -1)
    vmem = pl.BlockSpec(memory_space=pltpu.VMEM)
    hbm = pl.BlockSpec(memory_space=pltpu.HBM)
    dma = pltpu.SemaphoreType.DMA
    attended, base, memory = pl.pallas_call(
        functools.partial(kernel, lanes, nodes),
        out_shape=(
            jax.ShapeDtypeStruct((events, width), BF16),
            jax.ShapeDtypeStruct((events, width), F32),
            jax.ShapeDtypeStruct((owned, channels), F32),
        ),
        in_specs=[hbm] * 15,
        out_specs=(vmem, vmem, vmem),
        scratch_shapes=[
            pltpu.VMEM((2, events), jnp.int32),
            pltpu.VMEM((cap, nodes), jnp.int32),
            pltpu.VMEM((1, te), F32),
            pltpu.VMEM((1, te), F32),
            pltpu.VMEM((neighbours, events), jnp.int32),
            pltpu.VMEM((neighbours, events), jnp.int32),
            pltpu.VMEM((1, events), jnp.int32),
            pltpu.VMEM((1, channels), F32),
            pltpu.VMEM((owned, channels), F32),
            pltpu.VMEM(weight_message.shape, F32),
            pltpu.VMEM(weight_query.shape, BF16),
            pltpu.VMEM(weight_keyval.shape, BF16),
            pltpu.VMEM(weight_time.shape, BF16),
            pltpu.VMEM(weight_skip.shape, BF16),
            dma((15,)),
            pltpu.VMEM((lanes, 2, events), jnp.int32),
            pltpu.VMEM((nodes, 1, 128), jnp.int32),
            pltpu.VMEM((nodes, 1, 128), jnp.int32),
            pltpu.VMEM((nodes, cap, channels), BF16),
            pltpu.VMEM((nodes, cap, channels), BF16),
            pltpu.VMEM((lanes, owned, channels), F32),
            pltpu.VMEM((lanes, owned, te), F32),
            pltpu.VMEM((neighbours, te, events), F32),
            pltpu.VMEM((HEADS, 16, events), F32),
            pltpu.VMEM((HEADS, neighbours, 8, events), F32),
            pltpu.VMEM((HEADS, 16, events), F32),
            pltpu.VMEM((owned, channels), BF16),
            pltpu.VMEM((total + owned, width), BF16),
            pltpu.VMEM((RING * cap, HEADS * events), F32),
            pltpu.VMEM((total + owned, HEADS * events), BF16),
            pltpu.VMEM((HEADS * events, channels), BF16),
            dma((lanes,)),
            dma((lanes,)),
            dma((nodes,)),
            dma((nodes,)),
            dma((nodes,)),
            dma((nodes,)),
            pltpu.SemaphoreType.REGULAR,
        ],
        compiler_params=pltpu.CompilerParams(
            collective_id=0, has_side_effects=True, vmem_limit_bytes=56 * 1024 * 1024
        ),
    )(
        row(source_row), row(time_bucket), request_rows.T, row(time_frequency), row(time_phase), neighbour_age.T,
        neighbour_slot.T, row(neighbour_count), row(decay_rate), memory_start, weight_message, weight_query,
        weight_keyval, weight_time, weight_skip,
    )
    embedding, memory = pl.pallas_call(
        finish,
        out_shape=(
            jax.ShapeDtypeStruct((events, width), BF16),
            jax.ShapeDtypeStruct((owned, channels), F32),
        ),
        in_specs=[hbm] * 4,
        out_specs=(vmem, vmem),
        scratch_shapes=[
            pltpu.VMEM((events, width), BF16),
            pltpu.VMEM((events, width), F32),
            pltpu.VMEM(weight_output.shape, BF16),
            dma((5,)),
        ],
        compiler_params=pltpu.CompilerParams(vmem_limit_bytes=56 * 1024 * 1024),
    )(attended, base, memory, weight_output)
    return embedding, memory[None]


def solution(mesh):
    both, rows = P(("lane", "node")), P(("lane", "node"), None)
    return jax.shard_map(
        local,
        mesh=mesh,
        in_specs=(both, both, rows, rows, both, rows, P("node", None)) + (P(),) * 9,
        out_specs=(rows, P("lane", "node", None)),
        check_vma=False,
    )
```
